32 devices in a mesh: row: 4 (over y, x), col: 8 (over z, core).
Axes of the slice: x: 2, y: 2, z: 4, core: 2. Of those that a mesh axis runs over, the one named last changes fastest.
Arguments:
- owned_blocks: bfloat16 [1024, 8, 128, 128], P(('row', 'col')), may hold values from -0.8984375 to 0.8984375
- owned_rows: int32 [1024], P(('row', 'col')), may hold values from 0 to 64, as said below
- owned_cols: int32 [1024, 8], P(('row', 'col')), may hold values from 0 to 31
- keep: int32 [8, 256], P('row', 'col'), may hold values 0 or 1
Outputs:
- purified: bfloat16 [1024, 32768], P('row', 'col')
The draws below stay inside these ranges and needn't reach their ends.
Inputs may be any that keep to these rules, and one draw needn't show every extreme that they name: `owned_rows`: every block row of P stands in exactly one slot, in a slot of its own band; in every band some owner fills all 8 of its slots for that band.
All inputs are finite; a program needn't handle non-finite values. No bound on the sum of `keep` on one device may be relied on, other than what follows from the above.
Results may differ from the reference program's by a relative error of at most 0.005.
Values may be sent and summed in bfloat16 or wider, within the bound.
A program may use at most 256 MiB of HBM per device.

```python
import jax
import jax.numpy as jnp
from jax import lax

BLK = 128
GCOL = 32
RLOC = 2
NB = 256
HB = 64
W = 8
BANDCAP = 8
OWNSLOTS = 32
N_ROW = 4
N_COL = 8
DEVICES = 32


def draw_owned_rows(key, part):
    band_rows = 2 * GCOL
    full_count = band_rows // (2 * BANDCAP)
    remaining = band_rows - full_count * BANDCAP
    others = DEVICES - full_count
    base_share = remaining // others
    extra_share = remaining % others
    position = jnp.arange(DEVICES, dtype=jnp.int32)
    later = position - full_count
    counts = jnp.where(position < full_count, BANDCAP, base_share + (later < extra_share).astype(jnp.int32))
    starts = jnp.cumsum(counts) - counts
    slot_ids = jnp.arange(BANDCAP, dtype=jnp.int32)

    def one_band(band_id):
        band_key = jax.random.fold_in(key, 17 + band_id)
        owner_order = jax.random.permutation(jax.random.fold_in(band_key, 1), DEVICES)
        row_order = jax.random.permutation(jax.random.fold_in(band_key, 2), band_rows).astype(jnp.int32)
        spots = starts[:, None] + slot_ids[None, :]
        values = jnp.where(slot_ids[None, :] < counts[:, None], row_order[jnp.minimum(spots, band_rows - 1)], band_rows)
        return jnp.zeros((DEVICES, BANDCAP), jnp.int32).at[owner_order].set(values.astype(jnp.int32))
    tables = jax.vmap(one_band)(jnp.arange(N_ROW, dtype=jnp.int32))
    return tables.transpose(1, 0, 2).reshape(DEVICES * N_ROW * BANDCAP).astype(jnp.int32)


def with_ends(entries, key, least, top_value):
    place = [jax.random.randint(jax.random.fold_in(key, axis), (), 0, length) for axis, length in enumerate(entries.shape)]
    main_axis = entries.shape.index(max(entries.shape))
    next_to = place[:main_axis] + [(place[main_axis] + 1) % entries.shape[main_axis]] + place[main_axis + 1:]
    return entries.at[tuple(place)].set(least).at[tuple(next_to)].set(top_value)


def block_levels(stream_key, dims, split, least, largest):
    factor_of, own = 1.0, jax.random.fold_in(stream_key, 6)
    for dim, shards_of in split:
        draws = jnp.exp(jax.random.uniform(jax.random.fold_in(own, dim), (shards_of,), jnp.float32, least / len(split), largest / len(split)))
        factor_of = factor_of * jnp.repeat(draws, dims[dim] // shards_of).reshape([-1 if axis == dim else 1 for axis in range(len(dims))])
    return factor_of


def bell_draw(stream_key, dims, deviation, most, cuts=(), kind=jnp.bfloat16):
    array = jax.random.normal(stream_key, dims, jnp.float32) * deviation
    if len(cuts) > 0:
        array = block_levels(stream_key, dims, cuts, -0.22, 0.18) * array
    return jnp.clip(array, min=-most, max=most).astype(kind)


def setup_inputs(seed: int = 0) -> dict:
    seeds = jax.random.split(jax.random.key(seed), 5)
    owned_blocks = bell_draw(seeds[0], (DEVICES * OWNSLOTS, N_COL, BLK, BLK), 0.15, 0.8984375, ((0, 32),))
    owned_rows = draw_owned_rows(jax.random.fold_in(seeds[4], 71), 0)
    owned_cols = with_ends(jax.random.randint(seeds[2], (DEVICES * OWNSLOTS, N_COL), 0, GCOL), jax.random.fold_in(seeds[2], 1), 0, GCOL - 1).astype(jnp.int32)
    keep = with_ends((jax.random.randint(seeds[3], (W, NB), 0, 8) < 7).astype(jnp.int32), jax.random.fold_in(seeds[3], 1), 0, 1)
    return dict(owned_blocks=owned_blocks, owned_rows=owned_rows, owned_cols=owned_cols, keep=keep)


def build_matrix(owned_blocks, owned_rows, owned_cols):
    slot_count = owned_rows.shape[0]
    band_ids = (jnp.arange(slot_count).astype(jnp.int32) // BANDCAP) % N_ROW
    row_ids = GCOL * (band_ids + N_ROW * (owned_rows // GCOL)) + owned_rows % GCOL
    row_ids = jnp.where(owned_rows < HB, row_ids, NB).astype(jnp.int32)
    blocks = jnp.zeros((NB, N_COL, BLK, BLK), jnp.bfloat16).at[row_ids].set(owned_blocks, mode="drop")
    columns = jnp.zeros((NB, N_COL), jnp.int32).at[row_ids].set(owned_cols, mode="drop")
    return blocks, columns


def reference(owned_blocks, owned_rows, owned_cols, keep):
    blocks, columns = build_matrix(owned_blocks, owned_rows, owned_cols)
    group_base = (GCOL * jnp.arange(N_COL)).astype(jnp.int32)
    window_ids = jnp.arange(W).astype(jnp.int32)
    window = (GCOL * (window_ids // RLOC) + window_ids % RLOC).astype(jnp.int32)
    left_blocks = blocks[window].astype(jnp.float32)
    inner_rows = (group_base[None, :] + columns[window]).astype(jnp.int32)
    right_blocks = blocks[inner_rows].astype(jnp.float32)
    targets = (group_base[None, None, :] + columns[inner_rows]).astype(jnp.int32)
    products = jnp.einsum("wgab,wghbc->wghac", left_blocks, right_blocks, precision=lax.Precision.HIGHEST)
    row_index = jnp.broadcast_to(window_ids[:, None, None], targets.shape)
    square = jnp.zeros((W, NB, BLK, BLK), jnp.float32).at[row_index, targets].add(products)
    keep_mask = keep.astype(jnp.float32)[:, :, None, None]
    filtered = (square * keep_mask).astype(jnp.bfloat16)

    def add_row(running, inner_id):
        left_piece = lax.dynamic_index_in_dim(filtered, inner_id, 1, keepdims=False).astype(jnp.float32)
        right_piece = blocks[inner_id].astype(jnp.float32)
        partial_terms = jnp.einsum("wab,gbc->wgac", left_piece, right_piece, precision=lax.Precision.HIGHEST)
        spots = (group_base + columns[inner_id]).astype(jnp.int32)
        return running.at[:, spots].add(partial_terms), None

    cubed, _ = lax.scan(add_row, jnp.zeros((W, NB, BLK, BLK), jnp.float32), jnp.arange(NB).astype(jnp.int32))
    purified = (3.0 * filtered.astype(jnp.float32) - 2.0 * cubed).astype(jnp.bfloat16)
    return purified.transpose(0, 2, 1, 3).reshape(W * BLK, NB * BLK)
```

```python
import functools

import jax
import jax.numpy as jnp
from jax import lax
from jax.experimental import pallas as pl
from jax.experimental.pallas import tpu as pltpu
from jax.sharding import PartitionSpec as P

MESH = pl.DeviceIdType.MESH
ANY = pl.BlockSpec(memory_space=pl.ANY)
SMEM = pl.BlockSpec(memory_space=pltpu.SMEM)
VMEM = pl.BlockSpec(memory_space=pltpu.VMEM)
DMA = pltpu.SemaphoreType.DMA
BIG = 60 * 1024 * 1024


def remote_params(number):
    return pltpu.CompilerParams(collective_id=number, has_side_effects=True)


def spread_kernel(n_row, n_col, meta, owned, meta_all, sibling, send, recv, pair_send, pair_recv):
    r, c = lax.axis_index("row"), lax.axis_index("col")
    me = r * n_col + c
    devices = n_row * n_col
    barrier = pltpu.get_barrier_semaphore()

    def greet(i, carry):
        d = lax.rem(me + i, devices)
        pl.semaphore_signal(barrier, inc=1, device_id=(d // n_col, lax.rem(d, n_col)), device_id_type=MESH)
        return carry

    lax.fori_loop(1, devices, greet, 0)
    pl.semaphore_wait(barrier, devices - 1)
    z, k = c // 2, lax.rem(c, 2)
    other = 1 - k
    pair = pltpu.make_async_remote_copy(
        src_ref=owned.at[:, :, other], dst_ref=sibling, send_sem=pair_send, recv_sem=pair_recv,
        device_id=(r, 2 * z + other), device_id_type=MESH)
    pair.start()

    def copy_to(i):
        d = lax.rem(me + i, devices)
        return pltpu.make_async_remote_copy(
            src_ref=meta, dst_ref=meta_all.at[me], send_sem=send.at[i], recv_sem=recv.at[i],
            device_id=(d // n_col, lax.rem(d, n_col)), device_id_type=MESH)

    def begin(i, carry):
        copy_to(i).start()
        return carry

    def finish(i, carry):
        copy_to(i).wait()
        return carry

    lax.fori_loop(1, devices, begin, 0)
    lax.fori_loop(1, devices, finish, 0)
    pair.wait()


def along_z_kernel(nz, source, got, send, recv):
    r, c = lax.axis_index("row"), lax.axis_index("col")
    z, k = c // 2, lax.rem(c, 2)
    barrier = pltpu.get_barrier_semaphore()
    for step in range(1, nz):
        to = lax.rem(z + step, nz)
        pl.semaphore_signal(barrier, inc=1, device_id=(r, 2 * to + k), device_id_type=MESH)
    pl.semaphore_wait(barrier, nz - 1)
    copies = []
    for step in range(1, nz):
        to = lax.rem(z + step, nz)
        copies.append(pltpu.make_async_remote_copy(
            src_ref=source.at[to], dst_ref=got.at[z], send_sem=send.at[step], recv_sem=recv.at[step],
            device_id=(r, 2 * to + k), device_id_type=MESH))
    for copy in copies:
        copy.start()
    for copy in copies:
        copy.wait()


def in_plane_kernel(n_row, source, got, send, recv):
    r, c = lax.axis_index("row"), lax.axis_index("col")
    barrier = pltpu.get_barrier_semaphore()
    for step in range(1, n_row):
        pl.semaphore_signal(barrier, inc=1, device_id=(lax.rem(r + step, n_row), c), device_id_type=MESH)
    pl.semaphore_wait(barrier, n_row - 1)
    copies = []
    for step in range(1, n_row):
        to = lax.rem(r + step, n_row)
        copies.append(pltpu.make_async_remote_copy(
            src_ref=source.at[to], dst_ref=got.at[r], send_sem=send.at[step], recv_sem=recv.at[step],
            device_id=(to, c), device_id_type=MESH))
    for copy in copies:
        copy.start()
    for copy in copies:
        copy.wait()


def left_kernel(n_col, piece, got, send, recv):
    r, c = lax.axis_index("row"), lax.axis_index("col")
    barrier = pltpu.get_barrier_semaphore()
    for step in range(1, n_col):
        pl.semaphore_signal(barrier, inc=1, device_id=(r, lax.rem(c + step, n_col)), device_id_type=MESH)
    pl.semaphore_wait(barrier, n_col - 1)
    copies = []
    for step in range(1, n_col):
        copies.append(pltpu.make_async_remote_copy(
            src_ref=piece, dst_ref=got.at[c], send_sem=send.at[step], recv_sem=recv.at[step],
            device_id=(r, lax.rem(c + step, n_col)), device_id_type=MESH))
    for copy in copies:
        copy.start()
    for copy in copies:
        copy.wait()


def last_kernel(n_row, nz, source, filtered, got, every, send, recv, fsend, frecv, psend, precv):
    r, c = lax.axis_index("row"), lax.axis_index("col")
    z, k = c // 2, lax.rem(c, 2)
    mate = (r, 2 * z + 1 - k)
    barrier = pltpu.get_barrier_semaphore()
    for step in range(1, n_row):
        pl.semaphore_signal(barrier, inc=1, device_id=(lax.rem(r + step, n_row), c), device_id_type=MESH)
    for step in range(1, nz):
        pl.semaphore_signal(barrier, inc=1, device_id=(r, 2 * lax.rem(z + step, nz) + k), device_id_type=MESH)
    pl.semaphore_signal(barrier, inc=1, device_id=mate, device_id_type=MESH)
    pl.semaphore_wait(barrier, n_row + nz - 1)
    copies = []
    for step in range(1, nz):
        copies.append(pltpu.make_async_remote_copy(
            src_ref=filtered, dst_ref=every.at[c], send_sem=fsend.at[step], recv_sem=frecv.at[step],
            device_id=(r, 2 * lax.rem(z + step, nz) + k), device_id_type=MESH))
    plane = []
    for step in range(1, n_row):
        to = lax.rem(r + step, n_row)
        plane.append(pltpu.make_async_remote_copy(
            src_ref=source.at[to], dst_ref=got.at[r], send_sem=send.at[step], recv_sem=recv.at[step],
            device_id=(to, c), device_id_type=MESH))
    for copy in copies + plane:
        copy.start()
    pairs = [pltpu.make_async_remote_copy(
        src_ref=filtered, dst_ref=every.at[c], send_sem=psend.at[0], recv_sem=precv.at[0],
        device_id=mate, device_id_type=MESH)]
    pairs[0].start()
    for step in range(1, nz):
        copies[step - 1].wait_recv()
        origin = 2 * lax.rem(z - step + nz, nz) + k
        pair = pltpu.make_async_remote_copy(
            src_ref=every.at[origin], dst_ref=every.at[origin], send_sem=psend.at[step], recv_sem=precv.at[step],
            device_id=mate, device_id_type=MESH)
        pair.start()
        pairs.append(pair)
    for copy in copies:
        copy.wait_send()
    for pair in pairs:
        pair.wait()
    for copy in plane:
        copy.wait()


def pick(first, second, index, dest, sem):
    limit = first.shape[0]

    @pl.when(index < limit)
    def _():
        pltpu.make_async_copy(first.at[index], dest, sem).start()

    @pl.when(index >= limit)
    def _():
        pltpu.make_async_copy(second.at[index - limit], dest, sem).start()


def gather_kernel(index, first, second, out, sem):
    start = pl.program_id(0) * out.shape[0]

    def begin(i, carry):
        pick(first, second, index[start + i], out.at[i], sem)
        return carry

    lax.fori_loop(0, out.shape[0], begin, 0)
    pltpu.make_async_copy(out, out, sem).wait()


def gather(index, first, second):
    block = first.shape[-2:]
    count = index.shape[0]
    chunk = max(n for n in range(1, min(count, 512) + 1) if count % n == 0)
    return pl.pallas_call(
        gather_kernel,
        grid=(count // chunk,),
        out_shape=jax.ShapeDtypeStruct((count,) + block, first.dtype),
        in_specs=[SMEM, ANY, ANY], out_specs=pl.BlockSpec((chunk,) + block, lambda i: (i, 0, 0)),
        scratch_shapes=[DMA],
        compiler_params=pltpu.CompilerParams(vmem_limit_bytes=BIG),
    )(index, first.reshape((-1,) + block), second.reshape((-1,) + block))


def square_kernel(left_at, right_at, slot, keep, lefts, own_left, rights, own_rights, out, a, b, acc, sems):
    count = out.shape[0]

    def begin(i, carry):
        pick(lefts, own_left, left_at[i], a.at[i], sems.at[0])
        pick(rights, own_rights, right_at[i], b.at[i], sems.at[1])
        return carry

    lax.fori_loop(0, count, begin, 0)
    acc[...] = jnp.zeros_like(acc)
    pltpu.make_async_copy(a, a, sems.at[0]).wait()
    pltpu.make_async_copy(b, b, sems.at[1]).wait()

    def multiply(i, carry):
        acc[slot[i]] += jnp.dot(a[i], b[i], preferred_element_type=jnp.float32)
        return carry

    lax.fori_loop(0, count, multiply, 0)

    def write(i, carry):
        out[i] = (acc[i] * keep[i].astype(jnp.float32)).astype(out.dtype)
        return carry

    lax.fori_loop(0, count, write, 0)


def cubed_kernel(left_at, right_at, target, own_target, every, own, rights, own_rights, out, a, b, f, acc, sems):
    count = a.shape[0]
    windows = acc.shape[0]
    block = a.shape[-1]
    per_window = count // windows
    own_per_window = f.shape[0] // windows

    def begin(i, carry):
        pick(every, own, left_at[i], a.at[i], sems.at[0])
        pick(rights, own_rights, right_at[i], b.at[i], sems.at[1])
        return carry

    lax.fori_loop(0, count, begin, 0)
    mine = pltpu.make_async_copy(own, f, sems.at[2])
    mine.start()
    acc[...] = jnp.zeros_like(acc)
    pltpu.make_async_copy(a, a, sems.at[0]).wait()
    pltpu.make_async_copy(b, b, sems.at[1]).wait()
    mine.wait()
    for w in range(windows):
        def multiply(i, carry):
            e = w * per_window + i
            acc[w, target[e]] += jnp.dot(a[e], b[e], preferred_element_type=jnp.float32)
            return carry

        lax.fori_loop(0, per_window, multiply, 0)
    acc[...] = -2.0 * acc[...]
    for w in range(windows):
        def add(i, carry):
            e = w * own_per_window + i
            acc[w, own_target[e]] += 3.0 * f[e].astype(jnp.float32)
            return carry

        lax.fori_loop(0, own_per_window, add, 0)
    for w in range(windows):
        for j in range(acc.shape[1]):
            out[w * block:(w + 1) * block, j * block:(j + 1) * block] = acc[w, j].astype(out.dtype)


def running(mask):
    n = mask.shape[-1]
    before = (jnp.arange(n)[:, None] < jnp.arange(n)[None, :]).astype(jnp.bfloat16)
    flat = mask.reshape(-1, n).astype(jnp.bfloat16)
    return jnp.dot(flat, before, preferred_element_type=jnp.float32).astype(jnp.int32).reshape(mask.shape)


def local(owned_blocks, owned_rows, owned_cols, keep):
    n_row, n_col = lax.axis_size("row"), lax.axis_size("col")
    devices = n_row * n_col
    nz = n_col // 2
    r, c = lax.axis_index("row"), lax.axis_index("col")
    z, k = c // 2, lax.rem(c, 2)
    block = owned_blocks.shape[-1]
    dtype = owned_blocks.dtype
    slots = owned_rows.shape[0]
    per_band = slots // n_row
    windows, gcols = keep.shape
    nb = gcols * n_col
    size = slots * (1 + n_col)
    tall = -(-size // 1024) * 8
    one = (block, block)

    packed = jnp.concatenate([owned_rows[:, None], owned_cols], axis=1).reshape(-1)
    meta = jnp.pad(packed, (0, tall * 128 - size)).reshape(tall, 128)
    meta_all, sibling = pl.pallas_call(
        functools.partial(spread_kernel, n_row, n_col),
        out_shape=(jax.ShapeDtypeStruct((devices, tall, 128), jnp.int32),
                   jax.ShapeDtypeStruct((slots, nz) + one, dtype)),
        in_specs=[ANY, ANY], out_specs=(ANY, ANY),
        scratch_shapes=[DMA((devices,)), DMA((devices,)), DMA, DMA],
        compiler_params=remote_params(0),
    )(meta, owned_blocks.reshape((slots, nz, 2) + one))
    me = r * n_col + c
    is_me = jnp.arange(devices)[:, None] == me
    labels = jnp.where(is_me, packed[None, :], meta_all.reshape(devices, -1)[:, :size])
    labels = labels.reshape(devices * slots, 1 + n_col)
    rows, cols = labels[:, 0], labels[:, 1:]
    filled = rows < gcols * 2
    band = jnp.arange(devices * slots, dtype=jnp.int32) // per_band % n_row
    row_id = jnp.where(filled, gcols * (band + n_row * (rows // gcols)) + rows % gcols, nb)
    chips = devices // 2
    pool = 2 * slots
    filled_pool = filled.reshape(chips, pool)
    place = running(filled_pool)
    chip_count = filled_pool.sum(axis=1)
    hit = row_id[None, :] == jnp.arange(nb, dtype=jnp.int32)[:, None]

    def at_row(values):
        return jnp.sum(jnp.where(hit, values[None, :], 0), axis=1)

    chip = at_row(jnp.arange(devices * slots, dtype=jnp.int32) // pool)
    spot = at_row(place.reshape(-1))
    row_cols = jnp.sum(jnp.where(hit[:, :, None], cols[None, :, :], 0), axis=1)
    line, plane = chip // nz, chip % nz

    base = gcols * jnp.arange(n_col, dtype=jnp.int32)
    window = gcols * jnp.arange(n_row, dtype=jnp.int32)[:, None] + jnp.arange(windows, dtype=jnp.int32)[None, :]
    inner = base + row_cols[window]
    targets = base + row_cols[inner]
    every_row = jnp.arange(nb, dtype=jnp.int32)
    need1 = jnp.any(inner.reshape(n_row, -1, 1) == every_row, axis=1)
    need1 = need1 | jnp.any(window[:, :, None] == every_row, axis=1)
    need2 = jnp.any(targets.reshape(n_row, -1, 1) == every_row, axis=1)
    on_line = line[None, :] == jnp.arange(n_row, dtype=jnp.int32)[:, None]

    def ranks(need):
        both = need[:, None, :] & on_line[None, :, :]
        rank = jnp.sum(jnp.where(both, running(both), 0), axis=1)
        return rank, both.sum(axis=2).max()

    rank1, most1 = ranks(need1)
    rank2, most2 = ranks(need2)
    fits_chip = chip_count.max()

    inner_mine = inner[r].reshape(-1)
    targets_mine = targets[r].reshape(-1)
    cols_mine = lax.dynamic_index_in_dim(row_cols, c, 1, keepdims=False)
    square_target = cols_mine[inner_mine].reshape(windows, n_col)
    same = square_target[:, :, None] == square_target[:, None, :]
    first = jnp.argmax(same, axis=2).astype(jnp.int32)
    square_slot = (first + n_col * jnp.arange(windows, dtype=jnp.int32)[:, None]).reshape(-1)
    kept = jnp.take_along_axis(keep, square_target, axis=1).reshape(-1)
    cubed_target = cols_mine[targets_mine]
    entries = windows * n_col

    def run(caps, number):
        cap, cap1, cap2 = caps
        mine = lax.dynamic_index_in_dim(jnp.where(filled_pool, place, pool), r * nz + z, 0, keepdims=False)
        pick_slot = jnp.sum(
            jnp.where(mine[None, :] == jnp.arange(cap)[:, None], jnp.arange(pool, dtype=jnp.int32)[None, :], 0), axis=1)
        zs = jnp.arange(nz, dtype=jnp.int32)[:, None]
        at = pick_slot[None, :] % slots
        index = jnp.where(
            pick_slot[None, :] // slots == k, at * n_col + 2 * zs + k, slots * n_col + at * nz + zs)
        outgoing = gather(index.reshape(-1), owned_blocks, sibling).reshape((nz, cap) + one)
        got = pl.pallas_call(
            functools.partial(along_z_kernel, nz),
            out_shape=jax.ShapeDtypeStruct((nz, cap) + one, dtype),
            in_specs=[ANY], out_specs=ANY,
            scratch_shapes=[DMA((nz,)), DMA((nz,))],
            compiler_params=remote_params(number),
        )(outgoing)
        held_at = plane * cap + spot + jnp.where(plane == z, nz * cap, 0)

        def demand(need, rank, limit):
            sending = need & (line == r)[None, :]
            chosen = sending[:, None, :] & (rank[:, None, :] == jnp.arange(limit, dtype=jnp.int32)[None, :, None])
            where = jnp.sum(jnp.where(chosen, held_at[None, None, :], 0), axis=2)
            return gather(where.reshape(-1), got, outgoing).reshape((n_row, limit) + one)

        def found(rank, limit):
            return line * limit + rank[r] + jnp.where(line == r, n_row * limit, 0)

        send1 = demand(need1, rank1, cap1)
        got1 = pl.pallas_call(
            functools.partial(in_plane_kernel, n_row),
            out_shape=jax.ShapeDtypeStruct((n_row, cap1) + one, dtype),
            in_specs=[ANY], out_specs=ANY,
            scratch_shapes=[DMA((n_row,)), DMA((n_row,))],
            compiler_params=remote_params(number + 1),
        )(send1)
        found1 = found(rank1, cap1)
        window_mine = gcols * r + jnp.arange(windows, dtype=jnp.int32)
        left_mine = gather(found1[window_mine], got1, send1)
        lefts = pl.pallas_call(
            functools.partial(left_kernel, n_col),
            out_shape=jax.ShapeDtypeStruct((n_col, windows) + one, dtype),
            in_specs=[ANY], out_specs=ANY,
            scratch_shapes=[DMA((n_col,)), DMA((n_col,))],
            compiler_params=remote_params(number + 2),
        )(left_mine)
        ws = jnp.arange(windows, dtype=jnp.int32)[:, None]
        gs = jnp.arange(n_col, dtype=jnp.int32)[None, :]
        left_at = jnp.where(gs == c, n_col * windows + ws, gs * windows + ws).reshape(-1)
        filtered = pl.pallas_call(
            square_kernel,
            out_shape=jax.ShapeDtypeStruct((entries,) + one, dtype),
            in_specs=[SMEM] * 4 + [ANY] * 4, out_specs=VMEM,
            scratch_shapes=[pltpu.VMEM((entries,) + one, dtype), pltpu.VMEM((entries,) + one, dtype),
                            pltpu.VMEM((entries,) + one, jnp.float32), DMA((2,))],
            compiler_params=pltpu.CompilerParams(vmem_limit_bytes=BIG),
        )(left_at, found1[inner_mine], square_slot, kept, lefts.reshape((-1,) + one), left_mine,
          got1.reshape((-1,) + one), send1.reshape((-1,) + one))
        send2 = demand(need2, rank2, cap2)
        got2, every = pl.pallas_call(
            functools.partial(last_kernel, n_row, nz),
            out_shape=(jax.ShapeDtypeStruct((n_row, cap2) + one, dtype),
                       jax.ShapeDtypeStruct((n_col, entries) + one, dtype)),
            in_specs=[ANY, ANY], out_specs=(ANY, ANY),
            scratch_shapes=[DMA((n_row,)), DMA((n_row,)), DMA((nz,)), DMA((nz,)), DMA((nz,)), DMA((nz,))],
            compiler_params=remote_params(number + 3),
        )(send2, filtered)
        found2 = found(rank2, cap2)
        place3 = ws[:, :, None] * n_col + gs[:, :, None]
        groups = jnp.arange(n_col, dtype=jnp.int32)[None, None, :]
        left_at = jnp.where(groups == c, n_col * entries + place3, groups * entries + place3).reshape(-1)
        count = windows * n_col * n_col
        return pl.pallas_call(
            cubed_kernel,
            out_shape=jax.ShapeDtypeStruct((windows * block, gcols * block), dtype),
            in_specs=[SMEM] * 4 + [ANY] * 4, out_specs=VMEM,
            scratch_shapes=[pltpu.VMEM((count,) + one, dtype), pltpu.VMEM((count,) + one, dtype),
                            pltpu.VMEM((entries,) + one, dtype),
                            pltpu.VMEM((windows, gcols) + one, jnp.float32), DMA((3,))],
            compiler_params=pltpu.CompilerParams(vmem_limit_bytes=BIG),
        )(left_at, found2[targets_mine], cubed_target, square_target.reshape(-1), every.reshape((-1,) + one), filtered,
          got2.reshape((-1,) + one), send2.reshape((-1,) + one))

    most_demand = windows * n_col * n_col
    full = (pool, windows * (n_col + 1), min(most_demand, nb, n_col * slots))
    small = (pool // 2, windows * (n_col + 1) * 2 // 3, 5 * most_demand // (4 * n_row) if n_row == 4 else most_demand // 4)
    fits = (fits_chip <= small[0]) & (most1 <= small[1]) & (most2 <= small[2])
    return lax.cond(fits, lambda: run(small, 1), lambda: run(full, 5))


def solution(mesh):
    placed = (
        P(("row", "col"), None, None, None),
        P(("row", "col")),
        P(("row", "col"), None),
        P("row", "col"),
    )
    return jax.shard_map(
        local, mesh=mesh, in_specs=placed, out_specs=P("row", "col"), check_vma=False
    )
```

```python
import functools

import jax
import jax.numpy as jnp
from jax import lax
from jax.experimental import pallas as pl
from jax.experimental.pallas import tpu as pltpu
from jax.sharding import PartitionSpec as P

MESH = pl.DeviceIdType.MESH
ANY = pl.BlockSpec(memory_space=pl.ANY)
SMEM = pl.BlockSpec(memory_space=pltpu.SMEM)
VMEM = pl.BlockSpec(memory_space=pltpu.VMEM)
DMA = pltpu.SemaphoreType.DMA
BIG = 60 * 1024 * 1024


def remote_params(number):
    return pltpu.CompilerParams(collective_id=number, has_side_effects=True)


def spread_kernel(n_row, n_col, meta, owned, meta_all, sibling, send, recv, pair_send, pair_recv):
    r, c = lax.axis_index("row"), lax.axis_index("col")
    me = r * n_col + c
    devices = n_row * n_col
    barrier = pltpu.get_barrier_semaphore()

    def greet(i, carry):
        d = lax.rem(me + i, devices)
        pl.semaphore_signal(barrier, inc=1, device_id=(d // n_col, lax.rem(d, n_col)), device_id_type=MESH)
        return carry

    lax.fori_loop(1, devices, greet, 0)
    pl.semaphore_wait(barrier, devices - 1)
    z, k = c // 2, lax.rem(c, 2)
    other = 1 - k
    pair = pltpu.make_async_remote_copy(
        src_ref=owned.at[:, :, other], dst_ref=sibling, send_sem=pair_send, recv_sem=pair_recv,
        device_id=(r, 2 * z + other), device_id_type=MESH)
    pair.start()

    def copy_to(i):
        d = lax.rem(me + i, devices)
        return pltpu.make_async_remote_copy(
            src_ref=meta, dst_ref=meta_all.at[me], send_sem=send.at[i], recv_sem=recv.at[i],
            device_id=(d // n_col, lax.rem(d, n_col)), device_id_type=MESH)

    def begin(i, carry):
        copy_to(i).start()
        return carry

    def finish(i, carry):
        copy_to(i).wait()
        return carry

    lax.fori_loop(1, devices, begin, 0)
    lax.fori_loop(1, devices, finish, 0)
    pair.wait()


def greet(partners):
    barrier = pltpu.get_barrier_semaphore()
    for partner in partners:
        pl.semaphore_signal(barrier, inc=1, device_id=partner, device_id_type=MESH)
    pl.semaphore_wait(barrier, len(partners))


def send_to(source, dest, sems, step, partner):
    return pltpu.make_async_remote_copy(
        src_ref=source, dst_ref=dest, send_sem=sems[0].at[step], recv_sem=sems[1].at[step],
        device_id=partner, device_id_type=MESH)


def place_of(nz):
    r, c = lax.axis_index("row"), lax.axis_index("col")
    z, k = c // 2, lax.rem(c, 2)
    return r, c, z, k, [(r, 2 * lax.rem(z + step, nz) + k) for step in range(1, nz)]


def first_kernel(nz, count, source, got, send, recv):
    r, c, z, k, others = place_of(nz)
    greet(others)
    copies = [send_to(source.at[to[1] // 2, pl.ds(0, count)], got.at[z], (send, recv), step, to)
              for step, to in enumerate(others)]
    for copy in copies:
        copy.start()
    for copy in copies:
        copy.wait()


def second_kernel(n_row, nz, skip, source, wanted, got, plane_got, send, recv, psend, precv):
    r, c, z, k, others = place_of(nz)
    lines = [(lax.rem(r + step, n_row), c) for step in range(1, n_row)]
    greet(others + lines)
    count = got.shape[1]
    copies = [send_to(wanted.at[to[0]], plane_got.at[r], (psend, precv), step, to) for step, to in enumerate(lines)]
    copies += [send_to(source.at[to[1] // 2, pl.ds(skip, count)], got.at[z], (send, recv), step, to)
               for step, to in enumerate(others)]
    for copy in copies:
        copy.start()
    for copy in copies:
        copy.wait()


def left_kernel(nz, piece, got, send, recv, psend, precv):
    r, c, z, k, others = place_of(nz)
    mate = (r, 2 * z + 1 - k)
    greet(others + [mate])
    copies = [send_to(piece, got.at[c], (send, recv), step, to) for step, to in enumerate(others)]
    for copy in copies:
        copy.start()
    pairs = [send_to(piece, got.at[c], (psend, precv), 0, mate)]
    pairs[0].start()
    for step in range(1, nz):
        copies[step - 1].wait_recv()
        origin = 2 * lax.rem(z - step + nz, nz) + k
        pairs.append(send_to(got.at[origin], got.at[origin], (psend, precv), step, mate))
        pairs[-1].start()
    for copy in copies:
        copy.wait_send()
    for pair in pairs:
        pair.wait()


def last_kernel(n_row, nz, wanted, filtered, plane_got, every, send, recv, up_send, up_recv, down_send, down_recv,
                psend, precv):
    r, c, z, k, others = place_of(nz)
    mate = (r, 2 * z + 1 - k)
    barrier = pltpu.get_barrier_semaphore()
    lines = [(lax.rem(r + step, n_row), c) for step in range(1, n_row)]
    above, below = (r, 2 * lax.rem(z + 1, nz) + k), (r, 2 * lax.rem(z + nz - 1, nz) + k)
    greet(lines + [above, below, mate])
    plane = [send_to(wanted.at[to[0]], plane_got.at[r], (send, recv), step, to) for step, to in enumerate(lines)]

    def up(step, own):
        block = every.at[2 * lax.rem(z - step + nz, nz) + k]
        return send_to(filtered if own else block, block, (up_send, up_recv), step, above)

    def down(step, own):
        block = every.at[2 * lax.rem(z + step, nz) + k]
        return send_to(filtered if own else block, block, (down_send, down_recv), step, below)

    def across(step, own):
        block = every.at[2 * lax.rem(z + step, nz) + k]
        return send_to(filtered if own else block, block, (psend, precv), step, mate)

    @pl.when(z < nz - 1)
    def _():
        up(0, True).start()

    @pl.when(z > 0)
    def _():
        down(0, True).start()

    across(0, True).start()
    for copy in plane:
        copy.start()
    for step in range(1, nz):
        @pl.when(z - step >= 0)
        def _():
            up(step - 1, False).wait_recv()
            across(nz - step, False).start()

        @pl.when((z - step >= 0) & (z < nz - 1))
        def _():
            up(step, False).start()

        @pl.when(z + step <= nz - 1)
        def _():
            down(step - 1, False).wait_recv()
            across(step, False).start()

        @pl.when((z + step <= nz - 1) & (z > 0))
        def _():
            down(step, False).start()
    for step in range(nz):
        @pl.when((z - step >= 0) & (z < nz - 1))
        def _():
            up(step, False).wait_send()

        @pl.when((z + step <= nz - 1) & (z > 0))
        def _():
            down(step, False).wait_send()
    for step in range(nz):
        across(step, False).wait()
    for copy in plane:
        copy.wait()


def pick(sources, index, dest, sem):
    start = 0
    for source in sources:
        stop = start + source.shape[0]

        @pl.when((index >= start) & (index < stop))
        def _(source=source, start=start):
            pltpu.make_async_copy(source.at[index - start], dest, sem).start()

        start = stop


def gather_kernel(index, *refs):
    sources, (out, sem) = refs[:-2], refs[-2:]
    start = pl.program_id(0) * out.shape[0]

    def begin(i, carry):
        pick(sources, index[start + i], out.at[i], sem)
        return carry

    lax.fori_loop(0, out.shape[0], begin, 0)
    pltpu.make_async_copy(out, out, sem).wait()


def flat(array):
    return array.reshape((-1,) + array.shape[-2:])


def gather(index, *sources):
    block = sources[0].shape[-2:]
    count = index.shape[0]
    chunk = max(n for n in range(1, min(count, 512) + 1) if count % n == 0)
    return pl.pallas_call(
        gather_kernel,
        grid=(count // chunk,),
        out_shape=jax.ShapeDtypeStruct((count,) + block, sources[0].dtype),
        in_specs=[SMEM] + [ANY] * len(sources), out_specs=pl.BlockSpec((chunk,) + block, lambda i: (i, 0, 0)),
        scratch_shapes=[DMA],
        compiler_params=pltpu.CompilerParams(vmem_limit_bytes=BIG),
    )(index, *[flat(source) for source in sources])


def square_kernel(left_at, right_at, slot, keep, lefts, own_left, rights, own_rights, out, a, b, acc, sems):
    count = out.shape[0]

    def begin(i, carry):
        pick((lefts, own_left), left_at[i], a.at[i], sems.at[0])
        pick((rights, own_rights), right_at[i], b.at[i], sems.at[1])
        return carry

    lax.fori_loop(0, count, begin, 0)
    acc[...] = jnp.zeros_like(acc)
    pltpu.make_async_copy(a, a, sems.at[0]).wait()
    pltpu.make_async_copy(b, b, sems.at[1]).wait()

    def multiply(q, carry):
        ids = [q * 4 + i for i in range(4)]
        terms = [jnp.dot(a[i], b[i], preferred_element_type=jnp.float32) for i in ids]
        for i, term in zip(ids, terms):
            acc[slot[i]] += term
        return carry

    lax.fori_loop(0, count // 4, multiply, 0)

    def write(i, carry):
        out[i] = (acc[i] * keep[i].astype(jnp.float32)).astype(out.dtype)
        return carry

    lax.fori_loop(0, count, write, 0)


def cubed_kernel(left_at, right_at, target, own_target, every, own, got1, send1, got2, send2, out, a, b, f, acc, sems):
    count = a.shape[0]
    windows = acc.shape[0]
    block = a.shape[-1]
    per_window = count // windows
    own_per_window = f.shape[0] // windows
    mine = pltpu.make_async_copy(own, f, sems.at[2])
    mine.start()

    def begin(i, carry):
        pick((every, own), left_at[i], a.at[i], sems.at[0])
        pick((got1, send1, got2, send2), right_at[i], b.at[i], sems.at[1])
        return carry

    lax.fori_loop(0, count, begin, 0)
    acc[...] = jnp.zeros_like(acc)
    mine.wait()
    for w in range(windows):
        def add(i, carry):
            e = w * own_per_window + i
            acc[w, own_target[e]] -= 1.5 * f[e].astype(jnp.float32)
            return carry

        lax.fori_loop(0, own_per_window, add, 0)
    pltpu.make_async_copy(a, a, sems.at[0]).wait()
    pltpu.make_async_copy(b, b, sems.at[1]).wait()
    for w in range(windows):
        def multiply(q, carry):
            ids = [w * per_window + q * 4 + i for i in range(4)]
            terms = [jnp.dot(a[i], b[i], preferred_element_type=jnp.float32) for i in ids]
            for i, term in zip(ids, terms):
                acc[w, target[i]] += term
            return carry

        lax.fori_loop(0, per_window // 4, multiply, 0)
    for w in range(windows):
        for j in range(acc.shape[1]):
            out[w * block:(w + 1) * block, j * block:(j + 1) * block] = (-2.0 * acc[w, j]).astype(out.dtype)


def running(mask):
    n = mask.shape[-1]
    before = (jnp.arange(n)[:, None] < jnp.arange(n)[None, :]).astype(jnp.bfloat16)
    lines = mask.reshape(-1, n).astype(jnp.bfloat16)
    return jnp.dot(lines, before, preferred_element_type=jnp.float32).astype(jnp.int32).reshape(mask.shape)


def local(owned_blocks, owned_rows, owned_cols, keep):
    n_row, n_col = lax.axis_size("row"), lax.axis_size("col")
    devices = n_row * n_col
    nz = n_col // 2
    r, c = lax.axis_index("row"), lax.axis_index("col")
    z, k = c // 2, lax.rem(c, 2)
    block = owned_blocks.shape[-1]
    dtype = owned_blocks.dtype
    slots = owned_rows.shape[0]
    per_band = slots // n_row
    windows, gcols = keep.shape
    nb = gcols * n_col
    size = slots * (1 + n_col)
    tall = -(-size // 1024) * 8
    one = (block, block)
    chips = devices // 2
    pool = 2 * slots
    i32 = jnp.int32

    packed = jnp.concatenate([owned_rows[:, None], owned_cols], axis=1).reshape(-1)
    meta = jnp.pad(packed, (0, tall * 128 - size)).reshape(tall, 128)
    meta_all, sibling = pl.pallas_call(
        functools.partial(spread_kernel, n_row, n_col),
        out_shape=(jax.ShapeDtypeStruct((devices, tall, 128), i32),
                   jax.ShapeDtypeStruct((slots, nz) + one, dtype)),
        in_specs=[ANY, ANY], out_specs=(ANY, ANY),
        scratch_shapes=[DMA((devices,)), DMA((devices,)), DMA, DMA],
        compiler_params=remote_params(0),
    )(meta, owned_blocks.reshape((slots, nz, 2) + one))
    me = r * n_col + c
    is_me = jnp.arange(devices)[:, None] == me
    labels = jnp.where(is_me, packed[None, :], meta_all.reshape(devices, -1)[:, :size])
    labels = labels.reshape(devices * slots, 1 + n_col)
    rows, cols = labels[:, 0], labels[:, 1:]
    slot_ids = jnp.arange(devices * slots, dtype=i32)
    every_row = jnp.arange(nb, dtype=i32)
    filled = rows < gcols * 2
    row_id = jnp.where(filled, gcols * (slot_ids // per_band % n_row + n_row * (rows // gcols)) + rows % gcols, nb)
    holder = jnp.sum(jnp.where(row_id[None, :] == every_row[:, None], slot_ids[None, :], 0), axis=1)
    row_cols = cols[holder]
    chip = holder // pool
    line, plane = chip // nz, chip % nz

    base = gcols * jnp.arange(n_col, dtype=i32)
    window = gcols * jnp.arange(n_row, dtype=i32)[:, None] + jnp.arange(windows, dtype=i32)[None, :]
    inner = base + row_cols[window]
    targets = base + row_cols[inner]
    is_window = jnp.any(window[:, :, None] == every_row, axis=1)
    is_inner = jnp.any(inner.reshape(n_row, -1, 1) == every_row, axis=1) & ~is_window
    is_target = jnp.any(targets.reshape(n_row, -1, 1) == every_row, axis=1) & ~is_inner & ~is_window
    urgent = jnp.any(is_window | is_inner, axis=0)
    wanted_row = urgent.astype(i32) + jnp.any(is_window | is_inner | is_target, axis=0).astype(i32)
    wanted = jnp.where(filled, wanted_row[jnp.minimum(row_id, nb - 1)], 0).reshape(chips, pool)
    urgent_count = (wanted == 2).sum(axis=1)
    place = jnp.where(wanted == 2, running(wanted == 2), urgent_count[:, None] + running(wanted == 1))
    place = jnp.where(wanted > 0, place, pool)
    spot = place.reshape(-1)[holder]
    on_line = line[None, :] == jnp.arange(n_row, dtype=i32)[:, None]

    def ranks(need):
        both = need[:, None, :] & on_line[None, :, :]
        rank = jnp.sum(jnp.where(both, running(both), 0), axis=1)
        return rank, both.sum(axis=2).max()

    rank_window, _ = ranks(is_window)
    rank_inner, most_inner = ranks(is_inner)

    def shares(early, limit):
        now = is_target & (spot < early)[None, :]
        rank_now, _ = ranks(now)
        now = now & (rank_now < limit)
        later = is_target & ~now
        rank_later, most_later = ranks(later)
        return now, rank_now, later, rank_later, most_later

    inner_mine = inner[r].reshape(-1)
    targets_mine = targets[r].reshape(-1)
    cols_mine = lax.dynamic_index_in_dim(row_cols, c, 1, keepdims=False)
    square_target = cols_mine[inner_mine].reshape(windows, n_col)
    same = square_target[:, :, None] == square_target[:, None, :]
    first = jnp.argmax(same, axis=2).astype(i32)
    square_slot = (first + n_col * jnp.arange(windows, dtype=i32)[:, None]).reshape(-1)
    kept = jnp.take_along_axis(keep, square_target, axis=1).reshape(-1)
    cubed_target = cols_mine[targets_mine]
    entries = windows * n_col

    def run(caps, share, number):
        early, late, most, limit, rest = caps
        now, rank_now, later, rank_later, _ = share if share is not None else shares(early, limit)
        cap = early + late
        mine = lax.dynamic_index_in_dim(place, r * nz + z, 0, keepdims=False)
        pick_slot = jnp.sum(
            jnp.where(mine[None, :] == jnp.arange(cap)[:, None], jnp.arange(pool, dtype=i32)[None, :], 0), axis=1)
        zs = jnp.arange(nz, dtype=i32)[:, None]
        at = pick_slot[None, :] % slots
        index = jnp.where(
            pick_slot[None, :] // slots == k, at * n_col + 2 * zs + k, slots * n_col + at * nz + zs)
        outgoing = gather(index.reshape(-1), owned_blocks, sibling).reshape((nz, cap) + one)
        got_early = pl.pallas_call(
            functools.partial(first_kernel, nz, early),
            out_shape=jax.ShapeDtypeStruct((nz, early) + one, dtype),
            in_specs=[ANY], out_specs=ANY,
            scratch_shapes=[DMA((nz,)), DMA((nz,))],
            compiler_params=remote_params(number),
        )(outgoing)
        is_early = spot < early
        held_at = jnp.where(
            plane == z, nz * cap + plane * cap + spot,
            jnp.where(is_early, plane * early + spot, nz * early + plane * late + spot - early))
        early_at = jnp.where(plane == z, nz * early + plane * cap + spot, plane * early + spot)

        def demand(need, rank, count, source_at):
            sending = need & (line == r)[None, :]
            chosen = sending[:, None, :] & (rank[:, None, :] == jnp.arange(count, dtype=i32)[None, :, None])
            return jnp.sum(jnp.where(chosen, source_at[None, None, :], 0), axis=2)

        now_all = is_window | is_inner | now
        now_rank = jnp.where(is_window, rank_window, jnp.where(is_inner, windows + rank_inner, windows + most + rank_now))
        cap1 = windows + most + limit
        send1 = gather(demand(now_all, now_rank, cap1, early_at).reshape(-1), got_early, outgoing)
        send1 = send1.reshape((n_row, cap1) + one)
        got_late, got1 = pl.pallas_call(
            functools.partial(second_kernel, n_row, nz, early),
            out_shape=(jax.ShapeDtypeStruct((nz, late) + one, dtype),
                       jax.ShapeDtypeStruct((n_row, cap1) + one, dtype)),
            in_specs=[ANY, ANY], out_specs=(ANY, ANY),
            scratch_shapes=[DMA((nz,)), DMA((nz,)), DMA((n_row,)), DMA((n_row,))],
            compiler_params=remote_params(number + 1),
        )(outgoing, send1)
        found1 = line * cap1 + now_rank[r] + jnp.where(line == r, n_row * cap1, 0)
        window_mine = gcols * r + jnp.arange(windows, dtype=i32)
        left_mine = gather(found1[window_mine], got1, send1)
        lefts = pl.pallas_call(
            functools.partial(left_kernel, nz),
            out_shape=jax.ShapeDtypeStruct((n_col, windows) + one, dtype),
            in_specs=[ANY], out_specs=ANY,
            scratch_shapes=[DMA((nz,))] * 4,
            compiler_params=remote_params(number + 2),
        )(left_mine)
        ws = jnp.arange(windows, dtype=i32)[:, None]
        gs = jnp.arange(n_col, dtype=i32)[None, :]
        left_at = jnp.where(gs == c, n_col * windows + ws, gs * windows + ws).reshape(-1)
        filtered = pl.pallas_call(
            square_kernel,
            out_shape=jax.ShapeDtypeStruct((entries,) + one, dtype),
            in_specs=[SMEM] * 4 + [ANY] * 4, out_specs=VMEM,
            scratch_shapes=[pltpu.VMEM((entries,) + one, dtype), pltpu.VMEM((entries,) + one, dtype),
                            pltpu.VMEM((entries,) + one, jnp.float32), DMA((2,))],
            compiler_params=pltpu.CompilerParams(vmem_limit_bytes=BIG),
        )(left_at, found1[inner_mine], square_slot, kept, flat(lefts), left_mine, flat(got1), flat(send1))
        later_at = demand(later, rank_later, rest, held_at)
        send2 = gather(later_at.reshape(-1), got_early, got_late, outgoing).reshape((n_row, rest) + one)
        got2, every = pl.pallas_call(
            functools.partial(last_kernel, n_row, nz),
            out_shape=(jax.ShapeDtypeStruct((n_row, rest) + one, dtype),
                       jax.ShapeDtypeStruct((n_col, entries) + one, dtype)),
            in_specs=[ANY, ANY], out_specs=(ANY, ANY),
            scratch_shapes=[DMA((n_row,)), DMA((n_row,))] + [DMA((nz,))] * 6,
            compiler_params=remote_params(number + 3),
        )(send2, filtered)
        found2 = jnp.where(
            now_all[r], found1,
            2 * n_row * cap1 + line * rest + rank_later[r] + jnp.where(line == r, n_row * rest, 0))
        place3 = ws[:, :, None] * n_col + gs[:, :, None]
        groups = jnp.arange(n_col, dtype=i32)[None, None, :]
        left_at = jnp.where(groups == c, n_col * entries + place3, groups * entries + place3).reshape(-1)
        count = windows * n_col * n_col
        return pl.pallas_call(
            cubed_kernel,
            out_shape=jax.ShapeDtypeStruct((windows * block, gcols * block), dtype),
            in_specs=[SMEM] * 4 + [ANY] * 6, out_specs=VMEM,
            scratch_shapes=[pltpu.VMEM((count,) + one, dtype), pltpu.VMEM((count,) + one, dtype),
                            pltpu.VMEM((entries,) + one, dtype),
                            pltpu.VMEM((windows, gcols) + one, jnp.float32), DMA((3,))],
            compiler_params=pltpu.CompilerParams(vmem_limit_bytes=BIG),
        )(left_at, found2[targets_mine], cubed_target, square_target.reshape(-1), flat(every), filtered,
          flat(got1), flat(send1), flat(got2), flat(send2))

    most_demand = windows * n_col * n_col
    early, limit = 7 * pool // 32, most_demand // 8
    small = (early, early, 10 * entries // 16, limit, 22 * most_demand // 128)
    middle = (early, 26 * pool // 64, 12 * entries // 16, limit, most_demand // 4)
    full = (pool, 1, entries, limit, min(most_demand, nb, n_col * slots))
    share = shares(early, limit)
    most_pool, most_urgent = (wanted > 0).sum(axis=1).max(), urgent_count.max()

    def fits(caps):
        return ((most_pool <= caps[0] + caps[1]) & (most_urgent <= caps[0])
                & (most_inner <= caps[2]) & (share[-1] <= caps[4]))

    choice = jnp.where(fits(small), 0, jnp.where(fits(middle), 1, 2))
    return lax.switch(
        choice, [lambda: run(small, share, 1), lambda: run(middle, share, 5), lambda: run(full, None, 9)])


def solution(mesh):
    placed = (
        P(("row", "col"), None, None, None),
        P(("row", "col")),
        P(("row", "col"), None),
        P("row", "col"),
    )
    return jax.shard_map(
        local, mesh=mesh, in_specs=placed, out_specs=P("row", "col"), check_vma=False
    )
```

```python
import functools

import jax
import jax.numpy as jnp
from jax import lax
from jax.experimental import pallas as pl
from jax.experimental.pallas import tpu as pltpu
from jax.sharding import PartitionSpec as P

MESH = pl.DeviceIdType.MESH
ANY = pl.BlockSpec(memory_space=pl.ANY)
SMEM = pl.BlockSpec(memory_space=pltpu.SMEM)
VMEM = pl.BlockSpec(memory_space=pltpu.VMEM)
DMA = pltpu.SemaphoreType.DMA
BIG = 60 * 1024 * 1024


def remote_params(number):
    return pltpu.CompilerParams(collective_id=number, has_side_effects=True)


def spread_kernel(n_row, n_col, meta, owned, meta_all, sibling, send, recv, pair_send, pair_recv):
    r, c = lax.axis_index("row"), lax.axis_index("col")
    me = r * n_col + c
    devices = n_row * n_col
    barrier = pltpu.get_barrier_semaphore()

    def greet(i, carry):
        d = lax.rem(me + i, devices)
        pl.semaphore_signal(barrier, inc=1, device_id=(d // n_col, lax.rem(d, n_col)), device_id_type=MESH)
        return carry

    lax.fori_loop(1, devices, greet, 0)
    pl.semaphore_wait(barrier, devices - 1)
    z, k = c // 2, lax.rem(c, 2)
    other = 1 - k
    pair = pltpu.make_async_remote_copy(
        src_ref=owned.at[:, :, other], dst_ref=sibling, send_sem=pair_send, recv_sem=pair_recv,
        device_id=(r, 2 * z + other), device_id_type=MESH)
    pair.start()

    def copy_to(i):
        d = lax.rem(me + i, devices)
        return pltpu.make_async_remote_copy(
            src_ref=meta, dst_ref=meta_all.at[me], send_sem=send.at[i], recv_sem=recv.at[i],
            device_id=(d // n_col, lax.rem(d, n_col)), device_id_type=MESH)

    def begin(i, carry):
        copy_to(i).start()
        return carry

    def finish(i, carry):
        copy_to(i).wait()
        return carry

    lax.fori_loop(1, devices, begin, 0)
    lax.fori_loop(1, devices, finish, 0)
    pair.wait()


def greet(partners):
    barrier = pltpu.get_barrier_semaphore()
    for partner in partners:
        pl.semaphore_signal(barrier, inc=1, device_id=partner, device_id_type=MESH)
    pl.semaphore_wait(barrier, len(partners))


def send_to(source, dest, sems, step, partner):
    return pltpu.make_async_remote_copy(
        src_ref=source, dst_ref=dest, send_sem=sems[0].at[step], recv_sem=sems[1].at[step],
        device_id=partner, device_id_type=MESH)


def place_of(nz):
    r, c = lax.axis_index("row"), lax.axis_index("col")
    z, k = c // 2, lax.rem(c, 2)
    return r, c, z, k, [(r, 2 * lax.rem(z + step, nz) + k) for step in range(1, nz)]


def first_kernel(nz, count, source, got, send, recv):
    r, c, z, k, others = place_of(nz)
    greet(others)
    copies = [send_to(source.at[to[1] // 2, pl.ds(0, count)], got.at[z], (send, recv), step, to)
              for step, to in enumerate(others)]
    for copy in copies:
        copy.start()
    for copy in copies:
        copy.wait()


def second_kernel(n_row, nz, source, wanted, got, plane_got, send, recv, psend, precv):
    r, c, z, k, others = place_of(nz)
    lines = [(lax.rem(r + step, n_row), c) for step in range(1, n_row)]
    greet(others + lines)
    count = got.shape[1]
    copies = [send_to(wanted.at[to[0]], plane_got.at[r], (psend, precv), step, to) for step, to in enumerate(lines)]
    copies += [send_to(source.at[to[1] // 2, pl.ds(0, count)], got.at[z], (send, recv), step, to)
               for step, to in enumerate(others)]
    for copy in copies:
        copy.start()
    for copy in copies:
        copy.wait()


def left_kernel(nz, piece, got, send, recv, psend, precv):
    r, c, z, k, others = place_of(nz)
    mate = (r, 2 * z + 1 - k)
    greet(others + [mate])
    copies = [send_to(piece, got.at[c], (send, recv), step, to) for step, to in enumerate(others)]
    for copy in copies:
        copy.start()
    pairs = [send_to(piece, got.at[c], (psend, precv), 0, mate)]
    pairs[0].start()
    for step in range(1, nz):
        copies[step - 1].wait_recv()
        origin = 2 * lax.rem(z - step + nz, nz) + k
        pairs.append(send_to(got.at[origin], got.at[origin], (psend, precv), step, mate))
        pairs[-1].start()
    for copy in copies:
        copy.wait_send()
    for pair in pairs:
        pair.wait()


def last_kernel(n_row, nz, wanted, filtered, plane_got, every, send, recv, up_send, up_recv, down_send, down_recv,
                psend, precv):
    r, c, z, k, others = place_of(nz)
    mate = (r, 2 * z + 1 - k)
    lines = [(lax.rem(r + step, n_row), c) for step in range(1, n_row)]
    above, below = (r, 2 * lax.rem(z + 1, nz) + k), (r, 2 * lax.rem(z + nz - 1, nz) + k)
    greet(lines + [above, below, mate])
    plane = [send_to(wanted.at[to[0]], plane_got.at[r], (send, recv), step, to) for step, to in enumerate(lines)]

    def up(step, own):
        block = every.at[2 * lax.rem(z - step + nz, nz) + k]
        return send_to(filtered if own else block, block, (up_send, up_recv), step, above)

    def down(step, own):
        block = every.at[2 * lax.rem(z + step, nz) + k]
        return send_to(filtered if own else block, block, (down_send, down_recv), step, below)

    def across(step, own):
        block = every.at[2 * lax.rem(z + step, nz) + k]
        return send_to(filtered if own else block, block, (psend, precv), step, mate)

    @pl.when(z < nz - 1)
    def _():
        up(0, True).start()

    @pl.when(z > 0)
    def _():
        down(0, True).start()

    across(0, True).start()
    for copy in plane:
        copy.start()
    for step in range(1, nz):
        @pl.when(z - step >= 0)
        def _():
            up(step - 1, False).wait_recv()
            across(nz - step, False).start()

        @pl.when((z - step >= 0) & (z < nz - 1))
        def _():
            up(step, False).start()

        @pl.when(z + step <= nz - 1)
        def _():
            down(step - 1, False).wait_recv()
            across(step, False).start()

        @pl.when((z + step <= nz - 1) & (z > 0))
        def _():
            down(step, False).start()
    for step in range(nz):
        @pl.when((z - step >= 0) & (z < nz - 1))
        def _():
            up(step, False).wait_send()

        @pl.when((z + step <= nz - 1) & (z > 0))
        def _():
            down(step, False).wait_send()
    for step in range(nz):
        across(step, False).wait()
    for copy in plane:
        copy.wait()


def pick(sources, index, dest, sem):
    start = 0
    for source in sources:
        stop = start + source.shape[0]

        @pl.when((index >= start) & (index < stop))
        def _(source=source, start=start):
            pltpu.make_async_copy(source.at[index - start], dest, sem).start()

        start = stop


def gather_kernel(index, *refs):
    sources, (out, sem) = refs[:-2], refs[-2:]
    start = pl.program_id(0) * out.shape[0]

    def begin(i, carry):
        pick(sources, index[start + i], out.at[i], sem)
        return carry

    lax.fori_loop(0, out.shape[0], begin, 0)
    pltpu.make_async_copy(out, out, sem).wait()


def flat(array):
    return array.reshape((-1,) + array.shape[-2:])


def gather(index, *sources):
    block = sources[0].shape[-2:]
    count = index.shape[0]
    chunk = max(n for n in range(1, min(count, 512) + 1) if count % n == 0)
    return pl.pallas_call(
        gather_kernel,
        grid=(count // chunk,),
        out_shape=jax.ShapeDtypeStruct((count,) + block, sources[0].dtype),
        in_specs=[SMEM] + [ANY] * len(sources), out_specs=pl.BlockSpec((chunk,) + block, lambda i: (i, 0, 0)),
        scratch_shapes=[DMA],
        compiler_params=pltpu.CompilerParams(vmem_limit_bytes=BIG),
    )(index, *[flat(source) for source in sources])


def square_kernel(left_at, right_at, slot, keep, lefts, own_left, rights, own_rights, out, a, b, acc, sems):
    count = out.shape[0]

    def begin(i, carry):
        pick((lefts, own_left), left_at[i], a.at[i], sems.at[0])
        pick((rights, own_rights), right_at[i], b.at[i], sems.at[1])
        return carry

    lax.fori_loop(0, count, begin, 0)
    acc[...] = jnp.zeros_like(acc)
    pltpu.make_async_copy(a, a, sems.at[0]).wait()
    pltpu.make_async_copy(b, b, sems.at[1]).wait()

    def multiply(q, carry):
        ids = [q * 4 + i for i in range(4)]
        terms = [jnp.dot(a[i], b[i], preferred_element_type=jnp.float32) for i in ids]
        for i, term in zip(ids, terms):
            acc[slot[i]] += term
        return carry

    lax.fori_loop(0, count // 4, multiply, 0)

    def write(i, carry):
        out[i] = (acc[i] * keep[i].astype(jnp.float32)).astype(out.dtype)
        return carry

    lax.fori_loop(0, count, write, 0)


def cubed_kernel(left_at, right_at, target, own_target, every, own, got1, send1, got2, send2, out, a, b, f, acc, sems):
    count = a.shape[0]
    windows = acc.shape[0]
    block = a.shape[-1]
    per_window = count // windows
    own_per_window = f.shape[0] // windows
    mine = pltpu.make_async_copy(own, f, sems.at[2])
    mine.start()

    def begin(i, carry):
        pick((every, own), left_at[i], a.at[i], sems.at[0])
        pick((got1, send1, got2, send2), right_at[i], b.at[i], sems.at[1])
        return carry

    lax.fori_loop(0, count, begin, 0)
    acc[...] = jnp.zeros_like(acc)
    mine.wait()
    for w in range(windows):
        def add(i, carry):
            e = w * own_per_window + i
            acc[w, own_target[e]] -= 1.5 * f[e].astype(jnp.float32)
            return carry

        lax.fori_loop(0, own_per_window, add, 0)
    pltpu.make_async_copy(a, a, sems.at[0]).wait()
    pltpu.make_async_copy(b, b, sems.at[1]).wait()
    for w in range(windows):
        def multiply(q, carry):
            ids = [w * per_window + q * 4 + i for i in range(4)]
            terms = [jnp.dot(a[i], b[i], preferred_element_type=jnp.float32) for i in ids]
            for i, term in zip(ids, terms):
                acc[w, target[i]] += term
            return carry

        lax.fori_loop(0, per_window // 4, multiply, 0)
    for w in range(windows):
        for j in range(acc.shape[1]):
            out[w * block:(w + 1) * block, j * block:(j + 1) * block] = (-2.0 * acc[w, j]).astype(out.dtype)


def running(mask):
    n = mask.shape[-1]
    before = (jnp.arange(n)[:, None] < jnp.arange(n)[None, :]).astype(jnp.bfloat16)
    lines = mask.reshape(-1, n).astype(jnp.bfloat16)
    return jnp.dot(lines, before, preferred_element_type=jnp.float32).astype(jnp.int32).reshape(mask.shape)


def local(owned_blocks, owned_rows, owned_cols, keep):
    n_row, n_col = lax.axis_size("row"), lax.axis_size("col")
    devices = n_row * n_col
    nz = n_col // 2
    r, c = lax.axis_index("row"), lax.axis_index("col")
    z, k = c // 2, lax.rem(c, 2)
    block = owned_blocks.shape[-1]
    dtype = owned_blocks.dtype
    slots = owned_rows.shape[0]
    per_band = slots // n_row
    windows, gcols = keep.shape
    nb = gcols * n_col
    size = slots * (1 + n_col)
    tall = -(-size // 1024) * 8
    one = (block, block)
    chips = devices // 2
    pool = 2 * slots
    i32 = jnp.int32

    packed = jnp.concatenate([owned_rows[:, None], owned_cols], axis=1).reshape(-1)
    meta = jnp.pad(packed, (0, tall * 128 - size)).reshape(tall, 128)
    meta_all, sibling = pl.pallas_call(
        functools.partial(spread_kernel, n_row, n_col),
        out_shape=(jax.ShapeDtypeStruct((devices, tall, 128), i32),
                   jax.ShapeDtypeStruct((slots, nz) + one, dtype)),
        in_specs=[ANY, ANY], out_specs=(ANY, ANY),
        scratch_shapes=[DMA((devices,)), DMA((devices,)), DMA, DMA],
        compiler_params=remote_params(0),
    )(meta, owned_blocks.reshape((slots, nz, 2) + one))
    me = r * n_col + c
    is_me = jnp.arange(devices)[:, None] == me
    labels = jnp.where(is_me, packed[None, :], meta_all.reshape(devices, -1)[:, :size])
    labels = labels.reshape(devices * slots, 1 + n_col)
    rows, cols = labels[:, 0], labels[:, 1:]
    slot_ids = jnp.arange(devices * slots, dtype=i32)
    every_row = jnp.arange(nb, dtype=i32)
    filled = rows < gcols * 2
    row_id = jnp.where(filled, gcols * (slot_ids // per_band % n_row + n_row * (rows // gcols)) + rows % gcols, nb)
    holder = jnp.sum(jnp.where(row_id[None, :] == every_row[:, None], slot_ids[None, :], 0), axis=1)
    row_cols = cols[holder]
    chip = holder // pool
    line, plane = chip // nz, chip % nz

    base = gcols * jnp.arange(n_col, dtype=i32)
    window = gcols * jnp.arange(n_row, dtype=i32)[:, None] + jnp.arange(windows, dtype=i32)[None, :]
    inner = base + row_cols[window]
    targets = base + row_cols[inner]
    is_window = jnp.any(window[:, :, None] == every_row, axis=1)
    is_inner = jnp.any(inner.reshape(n_row, -1, 1) == every_row, axis=1) & ~is_window
    is_target = jnp.any(targets.reshape(n_row, -1, 1) == every_row, axis=1) & ~is_inner & ~is_window
    urgent = jnp.any(is_window | is_inner, axis=0)
    wanted_row = urgent.astype(i32) + jnp.any(is_window | is_inner | is_target, axis=0).astype(i32)
    wanted = jnp.sum(jnp.where(row_id[:, None] == every_row[None, :], wanted_row[None, :], 0), axis=1).reshape(chips, pool)
    urgent_count = (wanted == 2).sum(axis=1)
    place = jnp.where(wanted == 2, running(wanted == 2), urgent_count[:, None] + running(wanted == 1))
    place = jnp.where(wanted > 0, place, pool)
    spot = place.reshape(-1)[holder]
    on_line = line[None, :] == jnp.arange(n_row, dtype=i32)[:, None]

    def ranks(need):
        both = need[:, None, :] & on_line[None, :, :]
        rank = jnp.sum(jnp.where(both, running(both), 0), axis=1)
        return rank, both.sum(axis=2).max()

    rank_window, _ = ranks(is_window)
    rank_inner, most_inner = ranks(is_inner)

    def shares(early, limit):
        now = is_target & (spot < early)[None, :]
        rank_now, _ = ranks(now)
        now = now & (rank_now < limit)
        later = is_target & ~now
        rank_later, most_later = ranks(later)
        return now, rank_now, later, rank_later, most_later

    inner_mine = inner[r].reshape(-1)
    targets_mine = targets[r].reshape(-1)
    cols_mine = lax.dynamic_index_in_dim(row_cols, c, 1, keepdims=False)
    square_target = cols_mine[inner_mine].reshape(windows, n_col)
    same = square_target[:, :, None] == square_target[:, None, :]
    first = jnp.argmax(same, axis=2).astype(i32)
    square_slot = (first + n_col * jnp.arange(windows, dtype=i32)[:, None]).reshape(-1)
    kept = jnp.take_along_axis(keep, square_target, axis=1).reshape(-1)
    cubed_target = cols_mine[targets_mine]
    entries = windows * n_col

    step = (z - plane + nz) % nz
    zs = jnp.arange(nz, dtype=i32)[:, None]
    place_mine = lax.dynamic_index_in_dim(place, r * nz + z, 0, keepdims=False)

    def pooled(start, count):
        position = start + jnp.arange(count, dtype=i32)
        pick_slot = jnp.sum(
            jnp.where(place_mine[None, :] == position[:, None], jnp.arange(pool, dtype=i32)[None, :], 0), axis=1)
        at = pick_slot[None, :] % slots
        index = jnp.where(
            pick_slot[None, :] // slots == k, at * n_col + 2 * zs + k, slots * n_col + at * nz + zs)
        return gather(index.reshape(-1), owned_blocks, sibling).reshape((nz, count) + one)

    def demand(need, rank, count, source_at):
        sending = need & (line == r)[None, :]
        chosen = sending[:, None, :] & (rank[:, None, :] == jnp.arange(count, dtype=i32)[None, :, None])
        return jnp.sum(jnp.where(chosen, source_at[None, None, :], 0), axis=2)

    def opening(early, most, limit, share, parts):
        now, rank_now = share[:2]
        cap1 = windows + most + limit
        now_all = is_window | is_inner | now
        now_rank = jnp.where(is_window, rank_window, jnp.where(is_inner, windows + rank_inner, windows + most + rank_now))
        send1 = gather(demand(now_all, now_rank, cap1, step * early + spot).reshape(-1), *parts)
        found1 = line * cap1 + now_rank[r] + jnp.where(line == r, n_row * cap1, 0)
        return now_all, found1, send1.reshape((n_row, cap1) + one)

    def run(early, late, rest, share, parts, opened, outgoing, number):
        later, rank_later = share[2:4]
        now_all, found1, send1 = opened
        cap1 = send1.shape[1]
        late_at = jnp.where(plane == z, nz * late + plane * outgoing.shape[1], plane * late)
        held_at = jnp.where(spot < early, step * early + spot, nz * early + late_at + spot - early)
        got_late, got1 = pl.pallas_call(
            functools.partial(second_kernel, n_row, nz),
            out_shape=(jax.ShapeDtypeStruct((nz, late) + one, dtype),
                       jax.ShapeDtypeStruct((n_row, cap1) + one, dtype)),
            in_specs=[ANY, ANY], out_specs=(ANY, ANY),
            scratch_shapes=[DMA((nz,)), DMA((nz,)), DMA((n_row,)), DMA((n_row,))],
            compiler_params=remote_params(number + 1),
        )(outgoing, send1)
        window_mine = gcols * r + jnp.arange(windows, dtype=i32)
        left_mine = gather(found1[window_mine], got1, send1)
        lefts = pl.pallas_call(
            functools.partial(left_kernel, nz),
            out_shape=jax.ShapeDtypeStruct((n_col, windows) + one, dtype),
            in_specs=[ANY], out_specs=ANY,
            scratch_shapes=[DMA((nz,))] * 4,
            compiler_params=remote_params(number + 2),
        )(left_mine)
        ws = jnp.arange(windows, dtype=i32)[:, None]
        gs = jnp.arange(n_col, dtype=i32)[None, :]
        left_at = jnp.where(gs == c, n_col * windows + ws, gs * windows + ws).reshape(-1)
        filtered = pl.pallas_call(
            square_kernel,
            out_shape=jax.ShapeDtypeStruct((entries,) + one, dtype),
            in_specs=[SMEM] * 4 + [ANY] * 4, out_specs=VMEM,
            scratch_shapes=[pltpu.VMEM((entries,) + one, dtype), pltpu.VMEM((entries,) + one, dtype),
                            pltpu.VMEM((entries,) + one, jnp.float32), DMA((2,))],
            compiler_params=pltpu.CompilerParams(vmem_limit_bytes=BIG),
        )(left_at, found1[inner_mine], square_slot, kept, flat(lefts), left_mine, flat(got1), flat(send1))
        later_at = demand(later, rank_later, rest, held_at)
        send2 = gather(later_at.reshape(-1), *parts, got_late, outgoing).reshape((n_row, rest) + one)
        got2, every = pl.pallas_call(
            functools.partial(last_kernel, n_row, nz),
            out_shape=(jax.ShapeDtypeStruct((n_row, rest) + one, dtype),
                       jax.ShapeDtypeStruct((n_col, entries) + one, dtype)),
            in_specs=[ANY, ANY], out_specs=(ANY, ANY),
            scratch_shapes=[DMA((n_row,)), DMA((n_row,))] + [DMA((nz,))] * 6,
            compiler_params=remote_params(number + 3),
        )(send2, filtered)
        found2 = jnp.where(
            now_all[r], found1,
            2 * n_row * cap1 + line * rest + rank_later[r] + jnp.where(line == r, n_row * rest, 0))
        place3 = ws[:, :, None] * n_col + gs[:, :, None]
        groups = jnp.arange(n_col, dtype=i32)[None, None, :]
        left_at = jnp.where(groups == c, n_col * entries + place3, groups * entries + place3).reshape(-1)
        count = windows * n_col * n_col
        return pl.pallas_call(
            cubed_kernel,
            out_shape=jax.ShapeDtypeStruct((windows * block, gcols * block), dtype),
            in_specs=[SMEM] * 4 + [ANY] * 6, out_specs=VMEM,
            scratch_shapes=[pltpu.VMEM((count,) + one, dtype), pltpu.VMEM((count,) + one, dtype),
                            pltpu.VMEM((entries,) + one, dtype),
                            pltpu.VMEM((windows, gcols) + one, jnp.float32), DMA((3,))],
            compiler_params=pltpu.CompilerParams(vmem_limit_bytes=BIG),
        )(left_at, found2[targets_mine], cubed_target, square_target.reshape(-1), flat(every), filtered,
          flat(got1), flat(send1), flat(got2), flat(send2))

    most_demand = windows * n_col * n_col
    early, most, limit = 7 * pool // 32, 10 * entries // 16, most_demand // 8
    small = (early, 22 * most_demand // 128)
    middle = (26 * pool // 64, most_demand // 4)
    share = shares(early, limit)
    most_pool, most_urgent = (wanted > 0).sum(axis=1).max(), urgent_count.max()
    first_out = pooled(0, early)
    parts = [lax.dynamic_index_in_dim(first_out, z, 0, keepdims=False)]
    for by in range(1, nz):
        moved = lax.dynamic_index_in_dim(first_out, (z + by) % nz, 0, keepdims=False)
        parts.append(lax.ppermute(moved, "col", [(i, (i + 2 * by) % n_col) for i in range(n_col)]))
    late_out = pooled(early, middle[0])
    opened = opening(early, most, limit, share, parts)

    def usual(caps, number):
        return run(early, caps[0], caps[1], share, parts, opened, late_out, number)

    def widest(number):
        every_share = shares(pool, limit)
        outgoing = pooled(0, pool)
        got = pl.pallas_call(
            functools.partial(first_kernel, nz, pool),
            out_shape=jax.ShapeDtypeStruct((nz, pool) + one, dtype),
            in_specs=[ANY], out_specs=ANY,
            scratch_shapes=[DMA((nz,)), DMA((nz,))],
            compiler_params=remote_params(number),
        )(outgoing)
        held = [lax.dynamic_index_in_dim(outgoing, z, 0, keepdims=False)]
        held += [lax.dynamic_index_in_dim(got, (z - by + nz) % nz, 0, keepdims=False) for by in range(1, nz)]
        return run(pool, 1, min(most_demand, nb, n_col * slots), every_share, held,
                   opening(pool, entries, limit, every_share, held), outgoing, number)

    def fits(caps):
        return ((most_pool <= early + caps[0]) & (most_urgent <= early)
                & (most_inner <= most) & (share[-1] <= caps[1]))

    choice = jnp.where(fits(small), 0, jnp.where(fits(middle), 1, 2))
    return lax.switch(choice, [lambda: usual(small, 1), lambda: usual(middle, 5), lambda: widest(9)])


def solution(mesh):
    placed = (
        P(("row", "col"), None, None, None),
        P(("row", "col")),
        P(("row", "col"), None),
        P("row", "col"),
    )
    return jax.shard_map(
        local, mesh=mesh, in_specs=placed, out_specs=P("row", "col"), check_vma=False
    )
```
